128 devices in a mesh: tok: 16 (over z, y_lo, core), feat: 8 (over y_hi, x).
Axes of the slice: x: 4, y: 4 (y_hi: 2, y_lo: 2; y = y_hi * 2 + y_lo), z: 4, core: 2. Of those that a mesh axis runs over, the one named last changes fastest.
Arguments:
- teacher: float32 [8192, 16384], P('tok', 'feat'), may hold values from -720 to 720, as said below
- student: float32 [8192, 2048], P('tok', 'feat'), may hold values from -6 to 6
- gain: float32 [16384], P('feat'), may hold values from 0.1 to 1.9
- projector: float32 [2048, 16384], P(None, 'feat'), may hold values from -0.1875 to 0.1875
- momentum: float32 [2048, 16384], P('tok', 'feat'), may hold values from -0.12 to 0.12
Outputs:
- new_projector: float32 [2048, 16384], P('tok', 'feat')
- new_momentum: float32 [2048, 16384], P('tok', 'feat')
- student_grad: float32 [8192, 2048], P('tok', 'feat')
- loss_value: float32 [], replicated
The draws below stay inside these ranges and needn't reach their ends.
Inputs may be any that keep to these rules, and one draw needn't show every extreme that they name: `teacher`: finite real values.
All inputs are finite; a program needn't handle non-finite values.
Results may differ from the reference program's by a relative error of at most 0.00011.
Values sent between devices are 32-bit elements; how exact they have to be, the bound alone decides.
No kernel may reach another device: no remote copies, remote signals or barrier semaphores. Data moves between devices by JAX's collectives and lax.ppermute only.
A program may use at most 128 MiB of HBM per device.

```python
import math
import jax
import jax.numpy as jnp
from jax import lax

DS = 2048
DT = 16384
TOKENS = 8192


def draw_teacher(key, part):
    key_rows, key_cols, key_noise = jax.random.split(key, 3)
    row_part = jnp.exp(jax.random.uniform(key_rows, (TOKENS, 1), minval=0.0, maxval=math.log(10.0)))
    col_trend = jnp.exp(math.log(3.0) * jnp.arange(DT, dtype=jnp.float32) / DT)
    col_part = col_trend * jnp.exp(jax.random.uniform(key_cols, (DT,), minval=0.0, maxval=math.log(4.0)))
    noise_base = jnp.clip(jax.random.normal(key_noise, (TOKENS, DT)), -6.0, 6.0)
    return (row_part * col_part[None, :] * noise_base).astype(jnp.float32)


def with_spikes(drawn, rng, source, target, shards_of, factor):
    owner, partner = [(jnp.arange(drawn.shape[position]) // (drawn.shape[position] // shards_of)).reshape([-1 if axis == position else 1 for axis in range(drawn.ndim)]) for position in (source, target)]
    chosen = jax.random.permutation(rng, shards_of)[partner]
    strong = (owner == chosen) | (owner == (partner + shards_of // 2) % shards_of)
    return jnp.where(strong, factor * drawn, drawn)


def level_of(rng, extent, shards, smallest, top_value):
    factor_of, own = 1.0, jax.random.fold_in(rng, 6)
    for axis_at, parts in shards:
        heights = jnp.exp(jax.random.uniform(jax.random.fold_in(own, axis_at), (parts,), jnp.float32, smallest / len(shards), top_value / len(shards)))
        factor_of = factor_of * jnp.repeat(heights, extent[axis_at] // parts).reshape([-1 if axis == axis_at else 1 for axis in range(len(extent))])
    return factor_of


def noise(own_key, shape, spread, limit, pieces=(), kind=jnp.bfloat16):
    values = spread * jax.random.normal(own_key, shape, jnp.float32)
    if pieces:
        values = values * level_of(own_key, shape, pieces, -0.22, 0.18)
    return jnp.clip(values, -limit, limit).astype(kind)


def noise_with(rng, extent, deviation, limit, cuts, heavy, kind=jnp.bfloat16):
    array = deviation * jax.random.normal(rng, extent, jnp.float32)
    if cuts:
        array = array * level_of(rng, extent, cuts, -0.22, 0.18)
    return jnp.clip(with_spikes(array, jax.random.fold_in(rng, 3), *heavy), -limit, limit).astype(kind)


def setup_inputs(seed: int = 0) -> dict:
    key_list = jax.random.split(jax.random.key(seed), 6)
    teacher = draw_teacher(jax.random.fold_in(key_list[5], 71), 0)
    student = noise_with(key_list[1], (TOKENS, DS), 1.0, 6.0, ((0, 16), (1, 8)), (0, 1, 16, 2.0), jnp.float32)
    gain = jnp.clip(1.0 + 0.18 * jax.random.normal(key_list[2], (DT,), jnp.float32), 0.1, 1.9)
    projector = noise_with(key_list[3], (DS, DT), DS ** -0.5, 0.1875, ((1, 8),), (1, 0, 8, 2.0), jnp.float32)
    momentum = noise(key_list[4], (DS, DT), 0.02, 0.12, ((0, 16), (1, 8)), jnp.float32)
    return {"teacher": teacher, "student": student, "gain": gain, "projector": projector, "momentum": momentum}


norm_eps = 1e-05
momentum_rate = 0.9
step_rate = 0.5

def reference(teacher, student, gain, projector, momentum):
    highest = lax.Precision.HIGHEST
    row_total = lax.optimization_barrier(jnp.sum(teacher * teacher, axis=1, keepdims=True))
    row_scale = lax.rsqrt(row_total / DT + norm_eps)
    target = teacher * row_scale * gain[None, :]
    predicted = jnp.dot(student, projector, precision=highest, preferred_element_type=jnp.float32)
    residual = predicted - target
    loss_value = jnp.sum(residual * residual) / (TOKENS * DT)
    proj_grad = lax.dot_general(student, residual, (((0,), (0,)), ((), ())), precision=highest, preferred_element_type=jnp.float32) / TOKENS
    student_grad = lax.dot_general(residual, projector, (((1,), (1,)), ((), ())), precision=highest, preferred_element_type=jnp.float32)
    new_momentum = momentum_rate * momentum + proj_grad
    new_projector = projector - step_rate * new_momentum
    return (new_projector, new_momentum, student_grad, loss_value)
```

```python
import functools

import jax
import jax.numpy as jnp
from jax import lax
from jax.experimental import pallas as pl
from jax.experimental.pallas import tpu as pltpu
from jax.sharding import Mesh
from jax.sharding import PartitionSpec as P

DT = 16384
TOKENS = 8192
TOK = ("tok_0", "tok_1", "tok_2")
FEAT = ("feat_0", "feat_1")
Z, YLO, CORE, YHI, X = "tok_0", "tok_1", "tok_2", "feat_0", "feat_1"

norm_eps = 1e-05
momentum_rate = 0.9
step_rate = 0.5


F32, BF16 = jnp.float32, jnp.bfloat16
CY = 768
TN = 256
MIB = 1 << 20


def cost(flops, moved):
    return pl.CostEstimate(flops=flops, bytes_accessed=moved, transcendentals=0)


def halves(value):
    hi = value.astype(BF16)
    return hi, (value - hi.astype(F32)).astype(BF16)


def lhs3(hi, lo):
    return jnp.concatenate([hi, lo, hi], 1)


def rhs3(hi, lo, axis):
    return jnp.concatenate([hi, hi, lo], axis)


def dot(a, b, dims):
    return lax.dot_general(a, b, (dims, ((), ())), preferred_element_type=F32)


def shift(value, axis, by, size):
    return lax.ppermute(value, axis, [(i, (i + by) % size) for i in range(size)])


def sum_pair(value, axis, far=False):
    size = lax.axis_size(axis)
    step = 2 if far else 1
    return value + lax.ppermute(value, axis, [(i, i ^ step) for i in range(size)])


def after(index, *earlier):
    return lax.optimization_barrier((index, *earlier))[0]


def kernel(body, index, args, **spec):
    shapes = spec.pop("out_shape")
    grid_spec = pltpu.PrefetchScalarGridSpec(num_scalar_prefetch=1, **spec.pop("grid"))
    return pl.pallas_call(
        body,
        grid_spec=grid_spec,
        out_shape=shapes,
        compiler_params=pltpu.CompilerParams(vmem_limit_bytes=spec.pop("vmem") * MIB),
        **spec,
    )(index, *args)


FEATURE = {(dy, dx): dy * 4 + dx for dy in (0, 1) for dx in range(4)}
SLOT = {(dz, dy): 8 + dz * 2 + dy for dz in range(4) for dy in (0, 1)}
CORE_AT = 16


def table():
    z, ylo, core = lax.axis_index(Z), lax.axis_index(YLO), lax.axis_index(CORE)
    yhi, x = lax.axis_index(YHI), lax.axis_index(X)
    entries = [(yhi ^ dy) * 4 + (x + dx) % 4 for dy, dx in FEATURE]
    for dz, dy in SLOT:
        index = ((z + dz) % 4) * 2 + (ylo ^ dy)
        entries.append(((index // 4) ^ yhi) * 4 + (index % 4 - x) % 4)
    entries.append(core)
    return jnp.stack(entries).astype(jnp.int32)


EXTRA = 8


def pack_body(index, teacher, student, out, total):
    part = teacher[...]

    @pl.when(pl.program_id(0) == 0)
    def _():
        total[...] = jnp.zeros_like(total)

    squares = part * part
    folded = squares[:, :128]
    for k in range(1, part.shape[1] // 128):
        folded = folded + squares[:, k * 128 : (k + 1) * 128]
    total[...] += folded

    @pl.when(pl.program_id(0) == pl.num_programs(0) - 1)
    def _():
        half = student.shape[0] // 2
        sums = jnp.sum(total[...].T, axis=0, keepdims=True)
        for h in (0, 1):
            out[h, :half, :] = student[h * half : (h + 1) * half, :]
            out[h, half:, :] = jnp.broadcast_to(sums[:, h * half : (h + 1) * half], (EXTRA, half))


def packed(index, teacher, student):
    rows, cols = teacher.shape
    width = student.shape[1]
    shape = (2, rows // 2 + EXTRA, width)
    return kernel(
        pack_body,
        index,
        [teacher, student],
        grid=dict(
            grid=(4,),
            in_specs=[
                pl.BlockSpec((rows, cols // 4), lambda j, idx: (0, j)),
                pl.BlockSpec((rows, width), lambda j, idx: (0, 0)),
            ],
            out_specs=pl.BlockSpec(shape, lambda j, idx: (0, 0, 0)),
            scratch_shapes=[pltpu.VMEM((rows, 128), F32)],
        ),
        out_shape=jax.ShapeDtypeStruct(shape, F32),
        cost_estimate=cost(0, 4 * rows * cols),
        vmem=16,
    )


def forward_body(count, tile, with_acc, sums, *refs):
    refs = list(refs)
    refs.pop(0)
    blocks = [refs.pop(0) for _ in range(count)]
    parts = [refs.pop(0) for _ in range(count)]
    left, right = [], []
    half = blocks[0].shape[1] - EXTRA
    for k in range(count):
        block = jnp.concatenate([blocks[k][0, :half, :], blocks[k][1, :half, :]], 0)
        left.append(lhs3(*halves(block)))
        right.append(rhs3(*halves(parts[k][...]), 0))
    total = dot(jnp.concatenate(left, 1), jnp.concatenate(right, 0), ((1,), (0,)))
    if with_acc:
        total = total + refs.pop(0)[...]
    if not sums:
        refs[0][...] = total
        return
    partial = [refs.pop(0)[...] for _ in range(sums)]
    while len(partial) > 1:
        partial = [p + q for p, q in zip(partial[::2], partial[1::2])]
    teacher, gain, out, error = refs
    scale = lax.rsqrt(partial[0] / DT + norm_eps)
    scale = jnp.concatenate([scale[0].T, scale[1].T], 0)[:, :1]
    residual = total - (teacher[...] * scale) * gain[...]
    out[...] = residual

    @pl.when(pl.program_id(0) == 0)
    def _():
        error[...] = jnp.zeros_like(error)

    error[...] += jnp.sum((residual * residual).reshape(-1, 8, tile), axis=0)


def forward(index, pieces, at, projector, acc=None, final=None, first=0, tiles=4, tile=512):
    count = len(pieces)
    width = pieces[0].shape[2]
    half = pieces[0].shape[1] - EXTRA
    rows = 2 * half
    in_specs = [pl.BlockSpec(p.shape, lambda j, idx: (0, 0, 0)) for p in pieces]
    args = list(pieces)
    for k in range(count):
        args.append(projector)
        in_specs.append(
            pl.BlockSpec(
                (width, tile), functools.partial(lambda a, j, idx: (idx[a], j + first), at[k])
            )
        )
    if acc is not None:
        args.append(acc)
        in_specs.append(pl.BlockSpec((rows, tile), lambda j, idx: (0, j + first)))
    out_shape = jax.ShapeDtypeStruct((rows, tile * tiles), F32)
    out_specs = pl.BlockSpec((rows, tile), lambda j, idx: (0, j))
    sums = 0
    if final is not None:
        every, teacher, gain = final
        sums = len(every)
        args += [*every, teacher, gain]
        in_specs += [pl.BlockSpec((2, EXTRA, width), lambda j, idx: (0, half // EXTRA, 0))] * sums
        in_specs += [
            pl.BlockSpec((rows, tile), lambda j, idx: (0, j + first)),
            pl.BlockSpec((1, tile), lambda j, idx: (0, j + first)),
        ]
        out_shape = (out_shape, jax.ShapeDtypeStruct((8, tile), F32))
        out_specs = (out_specs, pl.BlockSpec((8, tile), lambda j, idx: (0, 0)))
    return kernel(
        functools.partial(forward_body, count, tile, acc is not None, sums),
        index,
        args,
        grid=dict(grid=(tiles,), in_specs=in_specs, out_specs=out_specs),
        out_shape=out_shape,
        cost_estimate=cost(6 * rows * width * count * tile * tiles, 8 * rows * tile * tiles),
        vmem=40,
    )


def prepare_body(count, slots, kept, *refs):
    refs = list(refs)
    refs.pop(0)
    own = [refs.pop(0) for _ in range(count)]
    other = [refs.pop(0) for _ in range(count)]
    if kept:
        old_hi, old_lo = refs.pop(0), refs.pop(0)
    hi, lo, sent = refs
    half = own[0].shape[1] - EXTRA
    if kept:
        for k in kept:
            hi[k] = old_hi[k]
            lo[k] = old_lo[k]
    for k in range(count):
        for h in (0, 1):
            rows = pl.ds(h * half, half)
            a, b = halves(own[k][h, :half, :].T)
            hi[slots[k], :, rows] = a
            lo[slots[k], :, rows] = b
            sent[k, rows, :] = other[k][h, :half, :]


def prepare(index, pieces, slots, old=None):
    count = len(pieces)
    _, long, width = pieces[0].shape
    rows = 2 * (long - EXTRA)
    in_specs = [
        pl.BlockSpec(
            (2, long, width // 2),
            functools.partial(lambda o, j, idx: (0, 0, idx[CORE_AT] ^ o), other),
        )
        for other in (0, 1)
        for _ in pieces
    ]
    args = [*pieces, *pieces]
    split = jax.ShapeDtypeStruct((8, width // 2, rows), BF16)
    sent = jax.ShapeDtypeStruct((count, rows, width // 2), F32)
    whole = [pl.BlockSpec(s.shape, lambda j, idx: (0, 0, 0)) for s in (split, split, sent)]
    kept = ()
    if old is not None:
        args += list(old)
        in_specs += whole[:2]
        kept = tuple(k for k in range(8) if k not in slots)
    return kernel(
        functools.partial(prepare_body, count, slots, kept),
        index,
        args,
        grid=dict(grid=(1,), in_specs=in_specs, out_specs=whole),
        out_shape=(split, split, sent),
        cost_estimate=cost(0, 8 * MIB),
        vmem=16,
    )


def turn_body(slots, index, first, second, hi, lo):
    for part, where in zip((first, second), slots):
        for k, slot in enumerate(where):
            a, b = halves(part[k].T)
            hi[slot], lo[slot] = a, b


def turned(index, came, slots):
    _, rows, width = came[0].shape
    split = jax.ShapeDtypeStruct((8, width, rows), BF16)
    spec = pl.BlockSpec((8, width, rows), lambda j, idx: (0, 0, 0))
    return kernel(
        functools.partial(turn_body, slots),
        index,
        came,
        grid=dict(
            grid=(1,),
            in_specs=[pl.BlockSpec(c.shape, lambda j, idx: (0, 0, 0)) for c in came],
            out_specs=(spec, spec),
        ),
        out_shape=(split, split),
        cost_estimate=cost(0, 4 * MIB),
        vmem=16,
    )


def grad_body(count, stacked, *refs):
    refs = list(refs)
    refs.pop(0)
    blocks = [[refs.pop(0)[0] for _ in range(count)] for _ in range(4)]
    mine, other = refs.pop(0)[...], refs.pop(0)[...]
    parts = [jnp.concatenate(part, 0) for part in blocks]
    left = jnp.concatenate([lhs3(*parts[:2]), lhs3(*parts[2:])], 1)
    right = jnp.concatenate([rhs3(*halves(mine), 0), rhs3(*halves(other), 0)], 0)
    total = dot(left, right, ((1,), (0,)))
    rows = total.shape[0] // count
    for k in range(count):
        if stacked:
            refs[0][k] = total[k * rows : (k + 1) * rows]
        else:
            refs[k][...] = total[k * rows : (k + 1) * rows]


def grad_blocks(index, at, splits, mine, other, stacked=False):
    count = len(at)
    _, rows, tokens = splits[0].shape
    cols = mine.shape[1]
    in_specs, args = [], []
    for part in splits:
        for k in range(count):
            args.append(part)
            in_specs.append(
                pl.BlockSpec(
                    (1, rows, tokens), functools.partial(lambda a, j, idx: (idx[a], 0, 0), at[k])
                )
            )
    in_specs += [pl.BlockSpec((tokens, TN), lambda j, idx: (0, j))] * 2
    if stacked:
        out = jax.ShapeDtypeStruct((count, rows, cols), F32)
        out_specs = pl.BlockSpec((count, rows, TN), lambda j, idx: (0, 0, j))
    else:
        out = [jax.ShapeDtypeStruct((rows, cols), F32)] * count
        out_specs = [pl.BlockSpec((rows, TN), lambda j, idx: (0, j))] * count
    return kernel(
        functools.partial(grad_body, count, stacked),
        index,
        [*args, mine, other],
        grid=dict(grid=(cols // TN,), in_specs=in_specs, out_specs=out_specs),
        out_shape=out,
        cost_estimate=cost(12 * rows * count * tokens * cols, 8 * tokens * cols),
        vmem=24,
    )


def state_body(count, split_at, index, part, res_y, res_z, *refs):
    outs, (hi, lo) = refs[:count], refs[count:]

    @pl.when(pl.program_id(0) == 0)
    def _():
        hi[:, :split_at], lo[:, :split_at] = halves(res_y[...])
        hi[:, split_at:], lo[:, split_at:] = halves(res_z[...])

    dims = ((1,), (1,))
    whi, wlo = halves(part[...])
    value = dot(hi[...], whi, dims) + (dot(lo[...], whi, dims) + dot(hi[...], wlo, dims))
    for k in range(count):

        @pl.when(pl.program_id(0) == k)
        def _(k=k):
            outs[k][...] = value


def state_blocks(index, at, projector, res_y, res_z):
    count = len(at)
    rows, split_at = res_y.shape
    cols, width = projector.shape[1], 256

    def which(j, idx):
        row = idx[at[0]]
        for k in range(1, count):
            row = jnp.where(j == k, idx[at[k]], row)
        return (row, 0)

    return kernel(
        functools.partial(state_body, count, split_at),
        index,
        [projector, res_y, res_z],
        grid=dict(
            grid=(count,),
            in_specs=[
                pl.BlockSpec((width, cols), which),
                pl.BlockSpec(res_y.shape, lambda j, idx: (0, 0)),
                pl.BlockSpec(res_z.shape, lambda j, idx: (0, 0)),
            ],
            out_specs=[pl.BlockSpec((rows, width), lambda j, idx: (0, 0))] * count,
            scratch_shapes=[pltpu.VMEM((rows, cols), BF16)] * 2,
        ),
        out_shape=[jax.ShapeDtypeStruct((rows, width), F32)] * count,
        cost_estimate=cost(6 * rows * count * width * cols, 8 * MIB),
        vmem=40,
    )


def in_layer(teacher, student, gain, projector, momentum):
    _, cols = teacher.shape
    width = student.shape[1]
    half = width // 2
    index = table()

    def at(*pairs):
        return [FEATURE[p] for p in pairs]

    own = packed(index, teacher, student)
    upper = shift(own, YHI, 1, 2)
    left, right = shift(own, X, 1, 4), shift(own, X, -1, 4)
    far = shift(own, X, 2, 4)
    acc = forward(index, [own], at((0, 0)), projector)
    acc = forward(after(index, acc), [upper], at((1, 0)), projector, acc)
    ul, ur = shift(upper, X, 1, 4), shift(upper, X, -1, 4)
    ufar = shift(far, YHI, 1, 2)
    acc = forward(after(index, acc), [left, right, far], at((0, 3), (0, 1), (0, 2)), projector, acc)
    hi, lo, sent_a = prepare(after(index, acc), [own, right, far, left], (0, 1, 2, 3))
    came_a = shift(sent_a, CORE, 1, 2)
    every = [own, far, left, right, upper, ufar, ul, ur]
    args = ([ul, ur, ufar], at((1, 3), (1, 1), (1, 2)), projector, acc)
    args += ((every, teacher, gain.reshape(1, cols)),)
    res_y, err_y = forward(after(index, sent_a), *args, 0, CY // TN, TN)
    other_y = shift(res_y, CORE, 1, 2)
    res_z, err_z = forward(after(index, res_y), *args, CY // TN, (cols - CY) // TN, TN)
    other_z = shift(res_z, CORE, 1, 2)
    error = jnp.sum(err_y + err_z).reshape(1)
    error = sum_pair(error, YHI)
    hi, lo, sent_b = prepare(after(index, res_z), [upper, ur, ufar, ul], (4, 5, 6, 7), (hi, lo))
    came_b = shift(sent_b, CORE, 1, 2)
    error = sum_pair(error, YLO)

    def state(index, *pairs):
        return state_blocks(index, at(*pairs), projector, res_y, res_z)

    sfar = state(after(index, sent_b), (0, 2), (1, 2))
    sfo, sft = shift(sfar[0], X, 1, 4), shift(sfar[1], X, -1, 4)
    splits = (
        hi,
        lo,
        *turned(after(index, sfar[0]), (came_a, came_b), ((0, 1, 2, 3), (4, 5, 6, 7))),
    )

    def grad_y(index, *pairs, stacked=False):
        return grad_blocks(index, [SLOT[p] for p in pairs], splits, res_y, other_y, stacked)

    def grad_z(index, *pairs):
        return grad_blocks(index, [SLOT[p] for p in pairs], splits, res_z, other_z)

    far_own, far_oth = grad_z(index, (2, 0), (2, 1))
    far_own_came, far_oth_came = shift(far_own, Z, 1, 4), shift(far_oth, Z, -1, 4)
    ys = grad_y(after(index, far_own, error), (2, 1), (1, 1), (3, 1), (0, 1), stacked=True)
    ys_came = shift(ys, YLO, 1, 2)
    error = sum_pair(error, CORE)
    up_own, up_oth, down_own, down_oth = grad_z(after(index, ys), (1, 0), (1, 1), (3, 0), (3, 1))
    s1o, s1t, s3o, s3t = state(after(index, up_own), (0, 1), (1, 1), (0, 3), (1, 3))
    up = shift(jnp.stack([up_own + far_own_came, up_oth]), Z, 1, 4)
    down = shift(jnp.stack([down_own, down_oth + far_oth_came]), Z, -1, 4)
    sup = shift(jnp.stack([s1o + sfo, s1t]), X, 1, 4)
    sdown = shift(jnp.stack([s3o, s3t + sft]), X, -1, 4)
    two, one, three, zero = grad_y(after(index, s1o), (2, 0), (1, 0), (3, 0), (0, 0))
    cut = half // 2
    two = two + ys_came[0]
    one, three = one + ys_came[1], three + ys_came[2]
    zero_own, zero_oth = grad_z(after(index, zero), (0, 0), (0, 1))
    s0o, s0t = state(after(index, zero_own), (0, 0), (1, 0))
    two, _ = lax.optimization_barrier((two, s0o))
    yfo, yft = shift(two[:cut], Z, 1, 4), shift(two[cut:], Z, -1, 4)
    z_came = shift(zero_oth + (up[1] + down[1]), YLO, 1, 2)
    yup = shift(jnp.concatenate([one[:cut] + yfo, one[cut:]], 0), Z, 1, 4)
    ydown = shift(jnp.concatenate([three[:cut], three[cut:] + yft], 0), Z, -1, 4)
    error = sum_pair(after(error, sup, sdown), X)
    error = sum_pair(error, X, far=True)
    s_came = shift(s0t + (sup[1] + sdown[1]), YHI, 1, 2)
    error = sum_pair(after(error, yup, ydown), Z)
    error = sum_pair(error, Z, far=True)
    grad_hi = (zero_own + (up[0] + down[0])) + z_came
    grad_lo = (zero + ys_came[3]) + (yup + ydown)
    proj_grad = jnp.concatenate([grad_lo, grad_hi], 1) / TOKENS
    student_grad = (s0o + (sup[0] + sdown[0])) + s_came
    loss_value = error[0] / (TOKENS * DT)

    new_momentum = momentum_rate * momentum + proj_grad
    own_block = lax.axis_index(Z) * 4 + lax.axis_index(YLO) * 2 + lax.axis_index(CORE)
    own_rows = lax.dynamic_slice_in_dim(projector, own_block * half, half, 0)
    new_projector = own_rows - step_rate * new_momentum
    return (new_projector, new_momentum, student_grad, loss_value)


def solution(mesh):
    split = Mesh(
        mesh.devices.reshape(4, 2, 2, 2, 4), ("tok_0", "tok_1", "tok_2", "feat_0", "feat_1")
    )
    in_specs = (P(TOK, FEAT), P(TOK, FEAT), P(FEAT), P(None, FEAT), P(TOK, FEAT))
    out_specs = (P(TOK, FEAT), P(TOK, FEAT), P(TOK, FEAT), P())
    return jax.shard_map(
        in_layer, mesh=split, in_specs=in_specs, out_specs=out_specs, check_vma=False
    )
```

```python
import functools

import jax
import jax.numpy as jnp
from jax import lax
from jax.experimental import pallas as pl
from jax.experimental.pallas import tpu as pltpu
from jax.sharding import Mesh
from jax.sharding import PartitionSpec as P

DT = 16384
TOKENS = 8192
TOK = ("tok_0", "tok_1", "tok_2")
FEAT = ("feat_0", "feat_1")
Z, YLO, CORE, YHI, X = "tok_0", "tok_1", "tok_2", "feat_0", "feat_1"

norm_eps = 1e-05
momentum_rate = 0.9
step_rate = 0.5


F32, BF16 = jnp.float32, jnp.bfloat16
CY = 768
TN = 256
MIB = 1 << 20


def halves(value):
    hi = value.astype(BF16)
    return hi, (value - hi.astype(F32)).astype(BF16)


def dot(a, b, dims):
    return lax.dot_general(a, b, (dims, ((), ())), preferred_element_type=F32)


def shift(value, axis, by, size):
    return lax.ppermute(value, axis, [(i, (i + by) % size) for i in range(size)])


def sum_pair(value, axis, far=False):
    size = lax.axis_size(axis)
    step = 2 if far else 1
    return value + lax.ppermute(value, axis, [(i, i ^ step) for i in range(size)])


def after(index, *earlier):
    return lax.optimization_barrier((index, *earlier))[0]


def kernel(body, index, args, out_shape, flops, scratch=(), vmem=8):
    specs = [pl.BlockSpec(memory_space=pltpu.SMEM)]
    specs += [pl.BlockSpec(memory_space=pltpu.VMEM)] * len(args)
    return pl.pallas_call(
        body,
        in_specs=specs,
        out_specs=[pl.BlockSpec(memory_space=pltpu.VMEM)] * len(out_shape),
        out_shape=out_shape,
        scratch_shapes=scratch,
        cost_estimate=pl.CostEstimate(flops=flops, bytes_accessed=MIB, transcendentals=0),
        compiler_params=pltpu.CompilerParams(vmem_limit_bytes=vmem * MIB),
    )(index, *args)


def of(shape, kind=F32):
    return jax.ShapeDtypeStruct(shape, kind)


FEATURE = {(dy, dx): dy * 4 + dx for dy in (0, 1) for dx in range(4)}
SLOT = {(dz, dy): 8 + dz * 2 + dy for dz in range(4) for dy in (0, 1)}
CORE_AT = 16


def table():
    z, ylo, core = lax.axis_index(Z), lax.axis_index(YLO), lax.axis_index(CORE)
    yhi, x = lax.axis_index(YHI), lax.axis_index(X)
    entries = [(yhi ^ dy) * 4 + (x + dx) % 4 for dy, dx in FEATURE]
    for dz, dy in SLOT:
        index = ((z + dz) % 4) * 2 + (ylo ^ dy)
        entries.append(((index // 4) ^ yhi) * 4 + (index % 4 - x) % 4)
    entries.append(core)
    return jnp.stack(entries).astype(jnp.int32)


EXTRA = 8


def packed(teacher, student):
    rows, width = student.shape
    sums = jnp.sum(teacher * teacher, axis=1).reshape(2, 1, rows // 2)
    sums = jnp.broadcast_to(sums, (2, EXTRA, rows // 2))
    return jnp.concatenate([student.reshape(2, rows // 2, width), sums], 1)


def forward_body(at, first, tiles, per, with_acc, final, index, *refs):
    refs = list(refs)
    count = len(at)
    blocks = [refs.pop(0) for _ in range(count)]
    projector = refs.pop(0)
    acc = refs.pop(0) if with_acc else None
    left = refs.pop()
    half = blocks[0].shape[1] - EXTRA
    width = blocks[0].shape[2]
    for k in range(count):
        for h in (0, 1):
            rows = pl.ds(h * half, half)
            for part, value in enumerate(halves(blocks[k][h, :half, :])):
                left[rows, pl.ds((2 * k + part) * width, width)] = value
    if final:
        sums = [refs.pop(0) for _ in range(8)]
        partial = [s[:, half:, :] for s in sums]
        while len(partial) > 1:
            partial = [p + q for p, q in zip(partial[::2], partial[1::2])]
        scale = lax.rsqrt(partial[0] / DT + norm_eps)
        scale = jnp.concatenate([scale[0].T, scale[1].T], 0)[:, :1]
        teacher, gain, out, out_hi, out_lo, error, column = refs
        column[...] = jnp.broadcast_to(scale, column.shape)
        error[...] = jnp.zeros_like(error)

    def product(cols):
        total = None
        for k in range(count):
            start = pl.multiple_of(index[at[k]] * width, width)
            b_hi, b_lo = halves(projector[pl.ds(start, width), cols])
            a_hi = left[:, pl.ds(2 * k * width, width)]
            a_lo = left[:, pl.ds((2 * k + 1) * width, width)]
            for a, b in ((a_hi, b_hi), (a_lo, b_hi), (a_hi, b_lo)):
                term = dot(a, b, ((1,), (0,)))
                total = term if total is None else total + term
        return total

    def step(j, carry):
        for p in range(per):
            here = pl.multiple_of((j * per + p) * TN, TN)
            there = pl.ds(here + first * TN, TN)
            here = pl.ds(here, TN)
            total = product(there)
            if with_acc:
                total = total + acc[:, there]
            if final:
                wide = jnp.concatenate([column[...]] * (TN // 128), 1)
                total = total - (teacher[:, there] * wide) * gain[:, there]
                out_hi[:, here], out_lo[:, here] = halves(total)
                out[:, here] = total
                error[...] += jnp.sum((total * total).reshape(-1, 8, TN), axis=0)
            else:
                refs[0][:, here] = total
        return carry

    lax.fori_loop(0, tiles // per, step, 0)


def forward(index, pieces, at, projector, acc=None, final=None, first=0, tiles=8, per=2):
    count = len(pieces)
    width = pieces[0].shape[2]
    rows = 2 * (pieces[0].shape[1] - EXTRA)
    args = [*pieces, projector]
    if acc is not None:
        args.append(acc)
    out = [of((rows, TN * tiles))]
    scratch = [pltpu.VMEM((rows, 2 * count * width), BF16)]
    if final is not None:
        every, teacher, gain = final
        args += [*every, teacher, gain]
        out += [of((rows, TN * tiles), BF16)] * 2 + [of((8, TN))]
        scratch.insert(0, pltpu.VMEM((rows, 128), F32))
    result = kernel(
        functools.partial(forward_body, at, first, tiles, per, acc is not None, final is not None),
        index,
        args,
        out,
        6 * rows * width * count * TN * tiles,
        scratch,
    )
    return result if final is not None else result[0]


def prepare_body(slots, kept, index, *refs):
    refs = list(refs)
    blocks = [refs.pop(0) for _ in slots]
    if kept:
        old_hi, old_lo = refs.pop(0), refs.pop(0)
    hi, lo, sent = refs
    half, width = blocks[0].shape[1] - EXTRA, blocks[0].shape[2] // 2
    for k in kept:
        hi[k] = old_hi[k]
        lo[k] = old_lo[k]
    mine = pl.ds(pl.multiple_of(index[CORE_AT] * width, width), width)
    theirs = pl.ds(pl.multiple_of((1 - index[CORE_AT]) * width, width), width)
    for k, slot in enumerate(slots):
        for h in (0, 1):
            rows = pl.ds(h * half, half)
            a, b = halves(blocks[k][h, :half, mine].T)
            hi[slot, :, rows] = a
            lo[slot, :, rows] = b
            sent[k, rows, :] = blocks[k][h, :half, theirs]


def prepare(index, pieces, slots, old=None):
    _, long, width = pieces[0].shape
    rows = 2 * (long - EXTRA)
    kept = () if old is None else tuple(k for k in range(8) if k not in slots)
    split = of((8, width // 2, rows), BF16)
    return kernel(
        functools.partial(prepare_body, slots, kept),
        index,
        [*pieces, *(old or ())],
        [split, split, of((len(pieces), rows, width // 2))],
        MIB,
    )


def turn_body(slots, index, first, second, hi, lo):
    for part, where in zip((first, second), slots):
        for k, slot in enumerate(where):
            a, b = halves(part[k].T)
            hi[slot], lo[slot] = a, b


def turned(index, came, slots):
    _, rows, width = came[0].shape
    split = of((8, width, rows), BF16)
    return kernel(functools.partial(turn_body, slots), index, came, [split, split], MIB)


def grad_body(at, places, adds, index, *refs):
    refs = list(refs)
    splits = [refs.pop(0) for _ in range(4)]
    mine_hi, mine_lo, other = (refs.pop(0) for _ in range(3))
    added = [refs.pop(0) for _ in adds]
    left, outs = refs.pop(), refs
    _, rows, tokens = splits[0].shape
    for k in range(len(at)):
        for part in range(4):
            where = pl.ds(k * rows, rows), pl.ds(part * tokens, tokens)
            left[where] = splits[part][index[at[k]]]

    def step(j, carry):
        cols = pl.ds(pl.multiple_of(j * TN, TN), TN)
        a_hi, a_lo, b_hi, b_lo = (left[:, pl.ds(p * tokens, tokens)] for p in range(4))
        own_hi, own_lo = mine_hi[:, cols], mine_lo[:, cols]
        oth_hi, oth_lo = halves(other[:, cols])
        total = None
        for a, b in (
            (a_hi, own_hi),
            (a_lo, own_hi),
            (a_hi, own_lo),
            (b_hi, oth_hi),
            (b_lo, oth_hi),
            (b_hi, oth_lo),
        ):
            term = dot(a, b, ((1,), (0,)))
            total = term if total is None else total + term
        for k, (out, row) in enumerate(places):
            value = total[k * rows : (k + 1) * rows]
            for (which, source), ref in zip(adds, added):
                if which == k:
                    value = value + (ref[:, cols] if source is None else ref[source, :, cols])
            if row is None:
                outs[out][:, cols] = value
            else:
                outs[out][row, :, cols] = value
        return carry

    lax.fori_loop(0, other.shape[1] // TN, step, 0)


def outputs_of(places, shape):
    out = []
    for k in range(1 + max(o for o, _ in places)):
        depth = sum(o == k for o, _ in places)
        single = any(o == k and r is None for o, r in places)
        out.append(of(shape if single else (depth, *shape)))
    return out


def grad_blocks(index, at, places, splits, mine, other, adds=()):
    _, rows, tokens = splits[0].shape
    cols = other.shape[1]
    which = tuple((k, row) for k, row, _ in adds)
    return kernel(
        functools.partial(grad_body, at, places, which),
        index,
        [*splits, *mine, other, *[array for _, _, array in adds]],
        outputs_of(places, (rows, cols)),
        12 * rows * len(at) * tokens * cols,
        [pltpu.VMEM((len(at) * rows, 4 * tokens), BF16)],
    )


def state_body(at, places, adds, split_at, width, index, projector, *refs):
    refs = list(refs)
    his = [refs.pop(0) for _ in range(2)]
    los = [refs.pop(0) for _ in range(2)]
    added = [refs.pop(0) for _ in adds]
    outs = refs
    cuts = (slice(0, split_at), slice(split_at, projector.shape[1]))
    for k, (out, row) in enumerate(places):
        rows = pl.ds(pl.multiple_of(index[at[k]] * width, width), width)
        total = None
        for cut, hi, lo in zip(cuts, his, los):
            w_hi, w_lo = halves(projector[rows, cut])
            for a, b in ((hi, w_hi), (lo, w_hi), (hi, w_lo)):
                term = dot(a[...], b, ((1,), (1,)))
                total = term if total is None else total + term
        for which, ref in zip(adds, added):
            if which == k:
                total = total + ref[...]
        if row is None:
            outs[out][...] = total
        else:
            outs[out][row] = total


def state_blocks(index, at, places, projector, his, los, adds=()):
    rows, split_at = his[0].shape
    width = 256
    which = tuple(k for k, _ in adds)
    return kernel(
        functools.partial(state_body, at, places, which, split_at, width),
        index,
        [projector, *his, *los, *[array for _, array in adds]],
        outputs_of(places, (rows, width)),
        6 * rows * len(at) * width * projector.shape[1],
    )


def in_layer(teacher, student, gain, projector, momentum):
    _, cols = teacher.shape
    width = student.shape[1]
    half = width // 2
    index = table()

    def at(*pairs):
        return [FEATURE[p] for p in pairs]

    own = packed(teacher, student)
    upper = shift(own, YHI, 1, 2)
    left, right = shift(own, X, 1, 4), shift(own, X, -1, 4)
    far = shift(own, X, 2, 4)
    acc = forward(index, [own], at((0, 0)), projector)
    acc = forward(after(index, acc), [upper], at((1, 0)), projector, acc)
    ul, ur = shift(upper, X, 1, 4), shift(upper, X, -1, 4)
    ufar = shift(far, YHI, 1, 2)
    acc = forward(after(index, acc), [left, right, far], at((0, 3), (0, 1), (0, 2)), projector, acc)
    hi, lo, sent_a = prepare(after(index, acc), [own, right, far, left], (0, 1, 2, 3))
    came_a = shift(sent_a, CORE, 1, 2)
    hi, lo, sent_b = prepare(after(index, sent_a), [upper, ur, ufar, ul], (4, 5, 6, 7), (hi, lo))
    came_b = shift(sent_b, CORE, 1, 2)
    every = [own, far, left, right, upper, ufar, ul, ur]
    args = ([ul, ur, ufar], at((1, 3), (1, 1), (1, 2)), projector, acc)
    args += ((every, teacher, gain.reshape(1, cols)),)
    res_z, *res_z_split, err_z = forward(
        after(index, sent_b), *args, CY // TN, (cols - CY) // TN, 1
    )
    other_z = shift(res_z, CORE, 1, 2)
    res_y, *res_y_split, err_y = forward(after(index, res_z), *args, 0, CY // TN, 1)
    other_y = shift(res_y, CORE, 1, 2)
    error = jnp.sum(err_y + err_z).reshape(1)
    error = sum_pair(error, Z)
    splits = (
        hi,
        lo,
        *turned(after(index, res_y), (came_a, came_b), ((0, 1, 2, 3), (4, 5, 6, 7))),
    )

    def state(index, pairs, places, adds=()):
        his, los = zip(res_y_split, res_z_split)
        return state_blocks(index, at(*pairs), places, projector, his, los, adds)

    def grad_y(index, pairs, places, adds=()):
        slots = [SLOT[p] for p in pairs]
        return grad_blocks(index, slots, places, splits, res_y_split, other_y, adds)

    def grad_z(index, pairs, places, adds=()):
        slots = [SLOT[p] for p in pairs]
        return grad_blocks(index, slots, places, splits, res_z_split, other_z, adds)

    apart = ((0, None), (1, None))
    paired = ((0, 0), (0, 1), (1, 0), (1, 1))
    sfar = state(after(index, splits[2]), ((0, 2), (1, 2)), apart)
    sfo, sft = shift(sfar[0], X, 1, 4), shift(sfar[1], X, -1, 4)
    error = sum_pair(after(error, sfar[0]), Z, far=True)
    zfar = grad_z(after(index, sfar[0]), ((2, 0), (2, 1)), apart)
    zfo, zft = shift(zfar[0], Z, 1, 4), shift(zfar[1], Z, -1, 4)
    error = sum_pair(after(error, zfar[0]), YLO)
    (ys,) = grad_y(
        after(index, zfar[0]), ((2, 1), (1, 1), (3, 1), (0, 1)), ((0, 0), (0, 1), (0, 2), (0, 3))
    )
    error = sum_pair(after(error, ys), YHI)
    zero = grad_z(after(index, ys), ((0, 0), (0, 1)), apart)
    ys, error, _ = lax.optimization_barrier((ys, error, zero[0]))
    ys = shift(ys, YLO, 1, 2)
    sup, sdown = state(
        after(index, zero[0]), ((0, 1), (1, 1), (0, 3), (1, 3)), paired, ((0, sfo), (3, sft))
    )
    sup_came, sdown_came = shift(sup, X, 1, 4), shift(sdown, X, -1, 4)
    up, down = grad_z(
        after(index, sup),
        ((1, 0), (1, 1), (3, 0), (3, 1)),
        paired,
        ((0, None, zfo), (3, None, zft)),
    )
    up_came, down_came = shift(up, Z, 1, 4), shift(down, Z, -1, 4)
    error = sum_pair(after(error, up), CORE)
    s0 = state(after(index, up), ((0, 0), (1, 0)), apart)
    two, one, three, rest = grad_y(
        after(index, s0[0]),
        ((2, 0), (1, 0), (3, 0), (0, 0)),
        ((0, None), (1, None), (2, None), (3, None)),
        tuple((k, k, ys) for k in range(4)),
    )
    s_part = s0[1] + (sup_came[1] + sdown_came[1])
    s_part, _ = lax.optimization_barrier((s_part, rest))
    s_came = shift(s_part, YHI, 1, 2)
    error = sum_pair(after(error, s_part), X)
    error = sum_pair(error, X, far=True)
    z_part = zero[1] + (up_came[1] + down_came[1])
    z_part, error, _ = lax.optimization_barrier((z_part, error, s_part))
    two, one, three, _ = lax.optimization_barrier((two, one, three, z_part))
    y2 = shift(two, Z, 2, 4)
    y1, y3 = shift(one, Z, 1, 4), shift(three, Z, -1, 4)
    z_came = shift(z_part, YLO, 1, 2)
    grad_hi = (zero[0] + (up_came[0] + down_came[0])) + z_came
    grad_lo = (rest + y2) + (y1 + y3)
    proj_grad = jnp.concatenate([grad_lo, grad_hi], 1) / TOKENS
    student_grad = (s0[0] + (sup_came[0] + sdown_came[0])) + s_came
    loss_value = error[0] / (TOKENS * DT)

    new_momentum = momentum_rate * momentum + proj_grad
    own_block = lax.axis_index(Z) * 4 + lax.axis_index(YLO) * 2 + lax.axis_index(CORE)
    own_rows = lax.dynamic_slice_in_dim(projector, own_block * half, half, 0)
    new_projector = own_rows - step_rate * new_momentum
    return (new_projector, new_momentum, student_grad, loss_value)


def solution(mesh):
    split = Mesh(
        mesh.devices.reshape(4, 2, 2, 2, 4), ("tok_0", "tok_1", "tok_2", "feat_0", "feat_1")
    )
    in_specs = (P(TOK, FEAT), P(TOK, FEAT), P(FEAT), P(None, FEAT), P(TOK, FEAT))
    out_specs = (P(TOK, FEAT), P(TOK, FEAT), P(TOK, FEAT), P())
    return jax.shard_map(
        in_layer, mesh=split, in_specs=in_specs, out_specs=out_specs, check_vma=False
    )
```

```python
import functools

import jax
import jax.numpy as jnp
from jax import lax
from jax.experimental import pallas as pl
from jax.experimental.pallas import tpu as pltpu
from jax.sharding import Mesh
from jax.sharding import PartitionSpec as P

DT = 16384
TOKENS = 8192
TOK = ("tok_0", "tok_1", "tok_2")
FEAT = ("feat_0", "feat_1")
Z, YLO, CORE, YHI, X = "tok_0", "tok_1", "tok_2", "feat_0", "feat_1"

norm_eps = 1e-05
momentum_rate = 0.9
step_rate = 0.5


F32, BF16 = jnp.float32, jnp.bfloat16
CY = 768
TN = 256
MIB = 1 << 20


def halves(value):
    hi = value.astype(BF16)
    return hi, (value - hi.astype(F32)).astype(BF16)


def dot(a, b, dims):
    return lax.dot_general(a, b, (dims, ((), ())), preferred_element_type=F32)


def shift(value, axis, by, size):
    return lax.ppermute(value, axis, [(i, (i + by) % size) for i in range(size)])


def sum_pair(value, axis, far=False):
    size = lax.axis_size(axis)
    step = 2 if far else 1
    return value + lax.ppermute(value, axis, [(i, i ^ step) for i in range(size)])


def after(index, *earlier):
    return lax.optimization_barrier((index, *earlier))[0]


def kernel(body, index, args, out_shape, flops, scratch=(), vmem=8):
    specs = [pl.BlockSpec(memory_space=pltpu.SMEM)]
    specs += [pl.BlockSpec(memory_space=pltpu.VMEM)] * len(args)
    return pl.pallas_call(
        body,
        in_specs=specs,
        out_specs=[pl.BlockSpec(memory_space=pltpu.VMEM)] * len(out_shape),
        out_shape=out_shape,
        scratch_shapes=scratch,
        cost_estimate=pl.CostEstimate(flops=flops, bytes_accessed=MIB, transcendentals=0),
        compiler_params=pltpu.CompilerParams(vmem_limit_bytes=vmem * MIB),
    )(index, *args)


def of(shape, kind=F32):
    return jax.ShapeDtypeStruct(shape, kind)


FEATURE = {(dy, dx): dy * 4 + dx for dy in (0, 1) for dx in range(4)}
SLOT = {(dz, dy): 8 + dz * 2 + dy for dz in range(4) for dy in (0, 1)}
CORE_AT = 16


def table():
    z, ylo, core = lax.axis_index(Z), lax.axis_index(YLO), lax.axis_index(CORE)
    yhi, x = lax.axis_index(YHI), lax.axis_index(X)
    entries = [(yhi ^ dy) * 4 + (x + dx) % 4 for dy, dx in FEATURE]
    for dz, dy in SLOT:
        index = ((z + dz) % 4) * 2 + (ylo ^ dy)
        entries.append(((index // 4) ^ yhi) * 4 + (index % 4 - x) % 4)
    entries.append(core)
    return jnp.stack(entries).astype(jnp.int32)


EXTRA = 8


def packed(teacher, student):
    rows, width = student.shape
    sums = jnp.sum(teacher * teacher, axis=1).reshape(2, 1, rows // 2)
    sums = jnp.broadcast_to(sums, (2, EXTRA, rows // 2))
    return jnp.concatenate([student.reshape(2, rows // 2, width), sums], 1)


def forward_body(at, first, tiles, per, with_acc, final, index, *refs):
    refs = list(refs)
    count = len(at)
    blocks = [refs.pop(0) for _ in range(count)]
    projector = refs.pop(0)
    acc = refs.pop(0) if with_acc else None
    left = refs.pop()
    half = blocks[0].shape[1] - EXTRA
    width = blocks[0].shape[2]
    for k in range(count):
        for h in (0, 1):
            rows = pl.ds(h * half, half)
            for part, value in enumerate(halves(blocks[k][h, :half, :])):
                left[rows, pl.ds((2 * k + part) * width, width)] = value
    if final:
        sums = [refs.pop(0) for _ in range(8)]
        partial = [s[:, half:, :] for s in sums]
        while len(partial) > 1:
            partial = [p + q for p, q in zip(partial[::2], partial[1::2])]
        scale = lax.rsqrt(partial[0] / DT + norm_eps)
        scale = jnp.concatenate([scale[0].T, scale[1].T], 0)[:, :1]
        teacher, gain, out, out_hi, out_lo, error, column = refs
        column[...] = jnp.broadcast_to(scale, column.shape)
        error[...] = jnp.zeros_like(error)

    def product(cols):
        total = None
        for k in range(count):
            start = pl.multiple_of(index[at[k]] * width, width)
            b_hi, b_lo = halves(projector[pl.ds(start, width), cols])
            a_hi = left[:, pl.ds(2 * k * width, width)]
            a_lo = left[:, pl.ds((2 * k + 1) * width, width)]
            for a, b in ((a_hi, b_hi), (a_lo, b_hi), (a_hi, b_lo)):
                term = dot(a, b, ((1,), (0,)))
                total = term if total is None else total + term
        return total

    def step(j, carry):
        for p in range(per):
            here = pl.multiple_of((j * per + p) * TN, TN)
            there = pl.ds(here + first * TN, TN)
            here = pl.ds(here, TN)
            total = product(there)
            if with_acc:
                total = total + acc[:, there]
            if final:
                wide = jnp.concatenate([column[...]] * (TN // 128), 1)
                total = total - (teacher[:, there] * wide) * gain[:, there]
                out_hi[:, here], out_lo[:, here] = halves(total)
                out[:, here] = total
                error[...] += jnp.sum((total * total).reshape(-1, 8, TN), axis=0)
            else:
                refs[0][:, here] = total
        return carry

    lax.fori_loop(0, tiles // per, step, 0)


def forward(index, pieces, at, projector, acc=None, final=None, first=0, tiles=8, per=2):
    count = len(pieces)
    width = pieces[0].shape[2]
    rows = 2 * (pieces[0].shape[1] - EXTRA)
    args = [*pieces, projector]
    if acc is not None:
        args.append(acc)
    out = [of((rows, TN * tiles))]
    scratch = [pltpu.VMEM((rows, 2 * count * width), BF16)]
    if final is not None:
        every, teacher, gain = final
        args += [*every, teacher, gain]
        out += [of((rows, TN * tiles), BF16)] * 2 + [of((8, TN))]
        scratch.insert(0, pltpu.VMEM((rows, 128), F32))
    result = kernel(
        functools.partial(forward_body, at, first, tiles, per, acc is not None, final is not None),
        index,
        args,
        out,
        6 * rows * width * count * TN * tiles,
        scratch,
    )
    return result if final is not None else result[0]


def prepare_body(slots, kept, index, *refs):
    refs = list(refs)
    blocks = [refs.pop(0) for _ in slots]
    if kept:
        old_hi, old_lo = refs.pop(0), refs.pop(0)
    hi, lo, sent = refs
    half, width = blocks[0].shape[1] - EXTRA, blocks[0].shape[2] // 2
    for k in kept:
        hi[k] = old_hi[k]
        lo[k] = old_lo[k]
    mine = pl.ds(pl.multiple_of(index[CORE_AT] * width, width), width)
    theirs = pl.ds(pl.multiple_of((1 - index[CORE_AT]) * width, width), width)
    for k, slot in enumerate(slots):
        for h in (0, 1):
            rows = pl.ds(h * half, half)
            a, b = halves(blocks[k][h, :half, mine].T)
            hi[slot, :, rows] = a
            lo[slot, :, rows] = b
            sent[k, rows, :] = blocks[k][h, :half, theirs]


def prepare(index, pieces, slots, old=None):
    _, long, width = pieces[0].shape
    rows = 2 * (long - EXTRA)
    kept = () if old is None else tuple(k for k in range(8) if k not in slots)
    split = of((8, width // 2, rows), BF16)
    return kernel(
        functools.partial(prepare_body, slots, kept),
        index,
        [*pieces, *(old or ())],
        [split, split, of((len(pieces), rows, width // 2))],
        MIB,
    )


def turn_body(slots, index, first, second, hi, lo):
    for part, where in zip((first, second), slots):
        for k, slot in enumerate(where):
            a, b = halves(part[k].T)
            hi[slot], lo[slot] = a, b


def turned(index, came, slots):
    _, rows, width = came[0].shape
    split = of((8, width, rows), BF16)
    return kernel(functools.partial(turn_body, slots), index, came, [split, split], MIB)


def grad_body(at, places, adds, index, *refs):
    refs = list(refs)
    splits = [refs.pop(0) for _ in range(4)]
    mine_hi, mine_lo, other = (refs.pop(0) for _ in range(3))
    added = [refs.pop(0) for _ in adds]
    left, outs = refs.pop(), refs
    _, rows, tokens = splits[0].shape
    for k in range(len(at)):
        for part in range(4):
            where = pl.ds(k * rows, rows), pl.ds(part * tokens, tokens)
            left[where] = splits[part][index[at[k]]]

    def step(j, carry):
        cols = pl.ds(pl.multiple_of(j * TN, TN), TN)
        a_hi, a_lo, b_hi, b_lo = (left[:, pl.ds(p * tokens, tokens)] for p in range(4))
        own_hi, own_lo = mine_hi[:, cols], mine_lo[:, cols]
        oth_hi, oth_lo = halves(other[:, cols])
        total = None
        for a, b in (
            (a_hi, own_hi),
            (a_lo, own_hi),
            (a_hi, own_lo),
            (b_hi, oth_hi),
            (b_lo, oth_hi),
            (b_hi, oth_lo),
        ):
            term = dot(a, b, ((1,), (0,)))
            total = term if total is None else total + term
        for k, (out, row) in enumerate(places):
            value = total[k * rows : (k + 1) * rows]
            for (which, source), ref in zip(adds, added):
                if which == k:
                    value = value + (ref[:, cols] if source is None else ref[source, :, cols])
            if row is None:
                outs[out][:, cols] = value
            else:
                outs[out][row, :, cols] = value
        return carry

    lax.fori_loop(0, other.shape[1] // TN, step, 0)


def outputs_of(places, shape):
    out = []
    for k in range(1 + max(o for o, _ in places)):
        depth = sum(o == k for o, _ in places)
        single = any(o == k and r is None for o, r in places)
        out.append(of(shape if single else (depth, *shape)))
    return out


def grad_blocks(index, at, places, splits, mine, other, adds=()):
    _, rows, tokens = splits[0].shape
    cols = other.shape[1]
    which = tuple((k, row) for k, row, _ in adds)
    return kernel(
        functools.partial(grad_body, at, places, which),
        index,
        [*splits, *mine, other, *[array for _, _, array in adds]],
        outputs_of(places, (rows, cols)),
        12 * rows * len(at) * tokens * cols,
        [pltpu.VMEM((len(at) * rows, 4 * tokens), BF16)],
    )


def state_body(at, places, adds, split_at, width, index, projector, *refs):
    refs = list(refs)
    his = [refs.pop(0) for _ in range(2)]
    los = [refs.pop(0) for _ in range(2)]
    added = [refs.pop(0) for _ in adds]
    outs = refs
    cuts = (slice(0, split_at), slice(split_at, projector.shape[1]))
    for k, (out, row) in enumerate(places):
        rows = pl.ds(pl.multiple_of(index[at[k]] * width, width), width)
        total = None
        for cut, hi, lo in zip(cuts, his, los):
            w_hi, w_lo = halves(projector[rows, cut])
            for a, b in ((hi, w_hi), (lo, w_hi), (hi, w_lo)):
                term = dot(a[...], b, ((1,), (1,)))
                total = term if total is None else total + term
        for which, ref in zip(adds, added):
            if which == k:
                total = total + ref[...]
        if row is None:
            outs[out][...] = total
        else:
            outs[out][row] = total


def state_blocks(index, at, places, projector, his, los, adds=()):
    rows, split_at = his[0].shape
    width = 256
    which = tuple(k for k, _ in adds)
    return kernel(
        functools.partial(state_body, at, places, which, split_at, width),
        index,
        [projector, *his, *los, *[array for _, array in adds]],
        outputs_of(places, (rows, width)),
        6 * rows * len(at) * width * projector.shape[1],
    )


def update_body(index, zero, up, down, z_came, rest, y1, y2, y3, momentum, own, new_own, new_momentum):
    for j in range(momentum.shape[1] // TN):
        cols = pl.ds(j * TN, TN)
        if j * TN < CY:
            grad = (rest[:, cols] + y2[:, cols]) + (y1[:, cols] + y3[:, cols])
        else:
            here = pl.ds(j * TN - CY, TN)
            grad = (zero[:, here] + (up[0, :, here] + down[0, :, here])) + z_came[:, here]
        updated = momentum_rate * momentum[:, cols] + grad / TOKENS
        new_momentum[:, cols] = updated
        new_own[:, cols] = own[:, cols] - step_rate * updated


def in_layer(teacher, student, gain, projector, momentum):
    _, cols = teacher.shape
    width = student.shape[1]
    half = width // 2
    index = table()

    def at(*pairs):
        return [FEATURE[p] for p in pairs]

    own = packed(teacher, student)
    upper = shift(own, YHI, 1, 2)
    left, right = shift(own, X, 1, 4), shift(own, X, -1, 4)
    far = shift(own, X, 2, 4)
    acc = forward(index, [own], at((0, 0)), projector)
    ul, ur = shift(upper, X, 1, 4), shift(upper, X, -1, 4)
    acc = forward(
        after(index, acc), [left, right, upper], at((0, 3), (0, 1), (1, 0)), projector, acc
    )
    ufar = shift(far, YHI, 1, 2)
    acc = forward(after(index, acc), [far], at((0, 2)), projector, acc)
    hi, lo, sent_a = prepare(after(index, acc), [own, right, far, left], (0, 1, 2, 3))
    came_a = shift(sent_a, CORE, 1, 2)
    hi, lo, sent_b = prepare(after(index, sent_a), [upper, ur, ufar, ul], (4, 5, 6, 7), (hi, lo))
    came_b = shift(sent_b, CORE, 1, 2)
    every = [own, far, left, right, upper, ufar, ul, ur]
    args = ([ul, ur, ufar], at((1, 3), (1, 1), (1, 2)), projector, acc)
    args += ((every, teacher, gain.reshape(1, cols)),)
    res_z, *res_z_split, err_z = forward(
        after(index, sent_b), *args, CY // TN, (cols - CY) // TN, 1
    )
    other_z = shift(res_z, CORE, 1, 2)
    res_y, *res_y_split, err_y = forward(after(index, res_z), *args, 0, CY // TN, 1)
    other_y = shift(res_y, CORE, 1, 2)
    error = jnp.sum(err_y + err_z).reshape(1)

    def state(index, pairs, places, adds=()):
        his, los = zip(res_y_split, res_z_split)
        return state_blocks(index, at(*pairs), places, projector, his, los, adds)

    apart = ((0, None), (1, None))
    paired = ((0, 0), (0, 1), (1, 0), (1, 1))
    sfar = state(after(index, res_y), ((0, 2), (1, 2)), apart)
    sfo, sft = shift(sfar[0], X, 1, 4), shift(sfar[1], X, -1, 4)
    splits = (
        hi,
        lo,
        *turned(after(index, sfar[0]), (came_a, came_b), ((0, 1, 2, 3), (4, 5, 6, 7))),
    )

    def grad_y(index, pairs, places, adds=()):
        slots = [SLOT[p] for p in pairs]
        return grad_blocks(index, slots, places, splits, res_y_split, other_y, adds)

    def grad_z(index, pairs, places, adds=()):
        slots = [SLOT[p] for p in pairs]
        return grad_blocks(index, slots, places, splits, res_z_split, other_z, adds)

    zfar = grad_z(after(index, splits[2]), ((2, 0), (2, 1)), apart)
    zfo, zft = shift(zfar[0], Z, 1, 4), shift(zfar[1], Z, -1, 4)
    (ys,) = grad_y(
        after(index, zfar[0]), ((2, 1), (1, 1), (3, 1), (0, 1)), ((0, 0), (0, 1), (0, 2), (0, 3))
    )
    ys_came = shift(ys, YLO, 1, 2)
    sup, sdown = state(
        after(index, ys), ((0, 1), (1, 1), (0, 3), (1, 3)), paired, ((0, sfo), (3, sft))
    )
    sup_came, sdown_came = shift(sup, X, 1, 4), shift(sdown, X, -1, 4)
    up, down = grad_z(
        after(index, sup),
        ((1, 0), (1, 1), (3, 0), (3, 1)),
        paired,
        ((0, None, zfo), (3, None, zft)),
    )
    up_came, down_came = shift(up, Z, 1, 4), shift(down, Z, -1, 4)
    error = sum_pair(after(error, up), CORE)
    s0 = state(after(index, up), ((0, 0), (1, 0)), apart)
    zero = grad_z(after(index, s0[0]), ((0, 0), (0, 1)), apart)
    error = sum_pair(after(error, zero[0]), YLO)
    two, one, three, rest = grad_y(
        after(index, zero[0]),
        ((2, 0), (1, 0), (3, 0), (0, 0)),
        ((0, None), (1, None), (2, None), (3, None)),
        tuple((k, k, ys_came) for k in range(4)),
    )
    error = sum_pair(after(error, rest), YHI)
    s_part = s0[1] + (sup_came[1] + sdown_came[1])
    s_part, _ = lax.optimization_barrier((s_part, rest))
    s_came = shift(s_part, YHI, 1, 2)
    error = sum_pair(after(error, up_came, down_came), Z)
    z_part = zero[1] + (up_came[1] + down_came[1])
    z_part, _ = lax.optimization_barrier((z_part, s_part))
    two, one, three, _ = lax.optimization_barrier((two, one, three, z_part))
    z_came = shift(z_part, YLO, 1, 2)
    y2 = shift(two, Z, 2, 4)
    y1, y3 = shift(one, Z, 1, 4), shift(three, Z, -1, 4)
    student_grad = (s0[0] + (sup_came[0] + sdown_came[0])) + s_came
    error = sum_pair(after(error, z_part, student_grad), X)
    error = sum_pair(error, X, far=True)
    error = sum_pair(after(error, y1, y2, y3), Z, far=True)
    loss_value = error[0] / (TOKENS * DT)

    own_block = lax.axis_index(Z) * 4 + lax.axis_index(YLO) * 2 + lax.axis_index(CORE)
    own_rows = lax.dynamic_slice_in_dim(projector, own_block * half, half, 0)
    new_projector, new_momentum = kernel(
        update_body,
        index,
        [zero[0], up_came, down_came, z_came, rest, y1, y2, y3, momentum, own_rows],
        [of(momentum.shape)] * 2,
        MIB,
    )
    return (new_projector, new_momentum, student_grad, loss_value)


def solution(mesh):
    split = Mesh(
        mesh.devices.reshape(4, 2, 2, 2, 4), ("tok_0", "tok_1", "tok_2", "feat_0", "feat_1")
    )
    in_specs = (P(TOK, FEAT), P(TOK, FEAT), P(FEAT), P(None, FEAT), P(TOK, FEAT))
    out_specs = (P(TOK, FEAT), P(TOK, FEAT), P(TOK, FEAT), P())
    return jax.shard_map(
        in_layer, mesh=split, in_specs=in_specs, out_specs=out_specs, check_vma=False
    )
```
